32 devices in a mesh: slab: 2 (over y), date: 4 (over z), rng: 2 (over x), az: 2 (over core).
Axes of the slice: x: 2, y: 2, z: 4, core: 2. Of those that a mesh axis runs over, the one named last changes fastest.
Arguments:
- slc: bfloat16 [64, 2, 128, 512], P(('slab', 'date'), None, 'az', 'rng'), parts along dimension 0, may hold values from -30 to 30
- lags: int32 [32, 6], P('date'), may hold values from 0 to 8, as said below
Outputs:
- coherence: bfloat16 [64, 6, 128, 512], P(('slab', 'date'), None, 'az', 'rng'), parts along dimension 0
- log_ratio: bfloat16 [64, 6, 128, 512], P(('slab', 'date'), None, 'az', 'rng'), parts along dimension 0
- quegan: float32 [64, 128, 512], P(('slab', 'date'), 'az', 'rng'), parts along dimension 0
The draws below stay inside these ranges and needn't reach their ends.
There are 2 independent parts, one for each index of `slab`. The reference program is written for one: setup_inputs(seed, part) draws one part's arguments, and reference() takes and returns one part's arrays. A program takes and returns all parts, laid end to end along the dimension named above; an argument that names none is the same for every part. Nothing has to cross between parts.
Inputs may be any that keep to these rules, and one draw needn't show every extreme that they name: Each entry is 0 (no partner) or a lag with date + lag < 32; the nonzero lags of one date are distinct; date 0 lists 6 partners, one of them at lag 8.
All inputs are finite; a program needn't handle non-finite values.
Results may differ from the reference program's by a relative error of at most 0.012.
Values may be sent and summed in bfloat16 or wider, within the bound.
A program may use at most 64 MiB of HBM per device.

```python
import jax
import jax.numpy as jnp
from jax import lax

SLOTS = 6
HALF_AZ = 2
HALF_RG = 10
LAG_MAX = 8
DATES = 32
LINES = 128
COLS = 512


def draw_slc(key, part):
    keys = jax.random.split(jax.random.fold_in(key, 11), 4)
    common = jnp.clip(jax.random.normal(keys[0], (1, 2, LINES, COLS), jnp.float32), -5.0, 5.0) * 0.7071
    own = jnp.clip(jax.random.normal(keys[1], (DATES, 2, LINES, COLS), jnp.float32), -5.0, 5.0) * 0.7071
    rho = jax.random.uniform(keys[2], (DATES, 1, 1, 1), jnp.float32, 0.3, 0.9)
    texture = jnp.exp(0.4 * jnp.clip(jax.random.normal(keys[3], (DATES, 1, LINES, COLS), jnp.float32), -3.0, 3.0))
    fields = texture * (jnp.sqrt(rho) * common + jnp.sqrt(1.0 - rho) * own)
    return jnp.clip(fields, -30.0, 30.0).astype(jnp.bfloat16)


def draw_lags(key, part):
    keys = jax.random.split(jax.random.fold_in(key, 23), 2)
    scores = jax.random.randint(keys[0], (DATES, LAG_MAX), 0, 1 << 20) * LAG_MAX + jnp.arange(LAG_MAX, dtype=jnp.int32)[None, :]
    order = jnp.argsort(scores, axis=1, stable=True)
    picked = (order[:, :SLOTS] + 1).astype(jnp.int32)
    counts = jax.random.randint(keys[1], (DATES, 1), 2, SLOTS + 1)
    slot_ids = jnp.arange(SLOTS, dtype=jnp.int32)[None, :]
    date_ids = jnp.arange(DATES, dtype=jnp.int32)[:, None]
    picked = jnp.where(date_ids == 0, LAG_MAX - slot_ids, picked)
    counts = jnp.where(date_ids == 0, SLOTS, counts)
    live_slots = (slot_ids < counts) & (date_ids + picked < DATES)
    return jnp.where(live_slots, picked, 0).astype(jnp.int32)


def setup_inputs(seed: int = 0, part: int = 0) -> dict:
    seeds = jax.random.split(jax.random.key(seed), 3)
    part_splits = jax.random.split(jax.random.fold_in(seeds[2], part), 3)
    return {
        "slc": draw_slc(jax.random.fold_in(jax.random.fold_in(seeds[2], part), 71), part),
        "lags": draw_lags(jax.random.fold_in(seeds[2], 71), part),
    }


EPS = 1e-5


def box_mean(fields):
    line_count = fields.shape[-2]
    column_count = fields.shape[-1]
    pad_width = [(0, 0)] * (fields.ndim - 2) + [(HALF_AZ, HALF_AZ), (HALF_RG, HALF_RG)]
    padded = jnp.pad(fields, pad_width)
    row_sums = padded[..., 0:line_count, :]
    for offset in range(1, 2 * HALF_AZ + 1):
        row_sums = row_sums + padded[..., offset:offset + line_count, :]
    totals = row_sums[..., :, 0:column_count]
    for offset in range(1, 2 * HALF_RG + 1):
        totals = totals + row_sums[..., :, offset:offset + column_count]
    return totals / float((2 * HALF_AZ + 1) * (2 * HALF_RG + 1))


def reference(slc, lags):
    fields = slc.astype(jnp.float32)
    powers = fields[:, 0] ** 2 + fields[:, 1] ** 2
    mean_power = lax.map(box_mean, powers) + EPS
    ratio_sum = jnp.sum(powers / mean_power, axis=0)
    quegan = mean_power * ratio_sum / float(DATES)

    def one_date(packed):
        date_index, lag_row = packed
        live_slots = lag_row > 0
        partners = (date_index + jnp.where(live_slots, lag_row, 0)).astype(jnp.int32)
        own_tile = fields[date_index]
        second = fields[partners]
        cross_re = own_tile[0][None] * second[:, 0] + own_tile[1][None] * second[:, 1]
        cross_im = own_tile[1][None] * second[:, 0] - own_tile[0][None] * second[:, 1]
        boxed_cross = box_mean(jnp.stack([cross_re, cross_im]))
        own_mean = mean_power[date_index][None]
        partner_mean = mean_power[partners]
        coherence = (boxed_cross[0] ** 2 + boxed_cross[1] ** 2) / (own_mean * partner_mean)
        log_ratio = jnp.log(own_mean / partner_mean)
        slot_mask = live_slots[:, None, None]
        return (jnp.where(slot_mask, coherence, 0.0).astype(jnp.bfloat16),
                jnp.where(slot_mask, log_ratio, 0.0).astype(jnp.bfloat16))

    coherence, log_ratio = lax.map(one_date, (jnp.arange(DATES, dtype=jnp.int32), lags))
    return coherence, log_ratio, quegan
```

```python
import functools

import jax
import jax.numpy as jnp
from jax import lax
from jax.experimental import pallas as pl
from jax.experimental.pallas import tpu as pltpu
from jax.sharding import PartitionSpec as P

HALF_AZ = 2
HALF_RG = 10
LAG_MAX = 8
EPS = 1e-05
LOOKS = float((2 * HALF_AZ + 1) * (2 * HALF_RG + 1))

LANES = 128
ROWS = 16
AHEAD_Z = 5
AHEAD_X = 2
F32 = jnp.float32
BF16 = jnp.bfloat16


def gather_kernel(sizes, slc, coh_out, log_out, mean_out, total_out,
                  tiles, band, coh, logs, inv, mean, acc, total, chain_out, chain_in,
                  own_sem, z_send, z_recv, x_send, x_recv, a_send, a_recv,
                  c_send, c_recv, out_sem):
    dates_axis, rng_axis, dates, lines, cols = sizes
    sides = 1 if rng_axis == 2 else 2
    date = lax.axis_index("date")
    rng = lax.axis_index("rng")
    az = lax.axis_index("az")
    has_next = date < dates_axis - 1
    has_prev = date > 0
    has_right = rng < rng_axis - 1
    has_left = rng > 0
    peer = 1 - az
    center = (slice(None), pl.ds(0, lines), pl.ds(0, cols))

    own = pltpu.make_async_copy(
        slc, tiles.at[pl.ds(0, dates), :, pl.ds(0, lines), pl.ds(0, cols)], own_sem)
    own.start()

    barrier = pltpu.get_barrier_semaphore()

    def greet(where):
        pl.semaphore_signal(barrier, inc=1, device_id=where, device_id_type=pl.DeviceIdType.MESH)

    greet({"az": peer})
    pl.when(has_prev)(lambda: greet({"date": date - 1}))
    pl.when(has_next)(lambda: greet({"date": date + 1}))
    pl.when(has_left)(lambda: greet({"rng": rng - 1}))
    pl.when(has_right)(lambda: greet({"rng": rng + 1}))

    col_out = lax.broadcasted_iota(jnp.int32, (cols, cols), 1)
    col_in = lax.broadcasted_iota(jnp.int32, (cols, cols), 0)
    band[0:cols, :] = (jnp.abs(col_in - col_out) <= HALF_RG).astype(F32).astype(BF16)
    edge_in = lax.broadcasted_iota(jnp.int32, (LANES, cols), 0)
    edge_out = lax.broadcasted_iota(jnp.int32, (LANES, cols), 1)
    for side in range(sides):
        if sides == 1:
            shift = (1 - rng) * cols - rng * LANES
        else:
            shift = -LANES if side == 0 else cols
        near = jnp.abs(edge_in + shift - edge_out) <= HALF_RG
        band[cols + side * LANES:cols + (side + 1) * LANES, :] = near.astype(F32).astype(BF16)

    peers = 1
    for cond in (has_prev, has_next, has_left, has_right):
        peers = peers + cond.astype(jnp.int32)
    pl.semaphore_wait(barrier, peers)

    def x_copy(e, src, side, to, start_col):
        block = cols + side * LANES
        if not isinstance(start_col, int):
            start_col = pl.multiple_of(start_col, LANES)
        return pltpu.make_async_remote_copy(
            src_ref=src.at[:, pl.ds(0, lines), pl.ds(start_col, LANES)],
            dst_ref=tiles.at[e, :, pl.ds(0, lines), pl.ds(block, LANES)],
            send_sem=x_send.at[side, e], recv_sem=x_recv.at[side, e],
            device_id={"rng": to}, device_id_type=pl.DeviceIdType.MESH)

    def x_each(e, src, act):
        if sides == 1:
            act(x_copy(e, src, 0, 1 - rng, (1 - rng) * (cols - LANES)))
        else:
            pl.when(has_right)(lambda: act(x_copy(e, src, 0, rng + 1, cols - LANES)))
            pl.when(has_left)(lambda: act(x_copy(e, src, 1, rng - 1, 0)))

    def x_wait(e):
        src = tiles.at[e]
        if sides == 1:
            x_copy(e, src, 0, 1 - rng, 0).wait_recv()
        else:
            pl.when(has_left)(lambda: x_copy(e, src, 0, rng - 1, 0).wait_recv())
            pl.when(has_right)(lambda: x_copy(e, src, 1, rng + 1, 0).wait_recv())

    row_src = (1 - az) * (lines - ROWS)

    def a_copy(e):
        return pltpu.make_async_remote_copy(
            src_ref=tiles.at[e, :, pl.ds(pl.multiple_of(row_src, ROWS), ROWS), :],
            dst_ref=tiles.at[e, :, pl.ds(lines, ROWS), :],
            send_sem=a_send.at[e], recv_sem=a_recv.at[e],
            device_id={"az": peer}, device_id_type=pl.DeviceIdType.MESH)

    def z_copy(k, to):
        return pltpu.make_async_remote_copy(
            src_ref=slc.at[k], dst_ref=tiles.at[(dates + k, *center)],
            send_sem=z_send.at[k], recv_sem=z_recv.at[k],
            device_id={"date": to}, device_id_type=pl.DeviceIdType.MESH)

    for k in range(dates):
        x_each(k, slc.at[k], lambda c: c.start())

    @pl.when(has_prev)
    def _():
        for k in range(dates):
            z_copy(k, date - 1).start()

    if sides == 2:
        zeros = jnp.zeros((2 * dates, 2, lines, LANES), BF16)

        @pl.when(rng == 0)
        def _():
            tiles[:, :, 0:lines, cols:cols + LANES] = zeros

        @pl.when(rng == rng_axis - 1)
        def _():
            tiles[:, :, 0:lines, cols + LANES:cols + 2 * LANES] = zeros

    own.wait()

    top = az.astype(F32)
    bottom = 1.0 - top

    def line_sums(y):
        ext = jnp.concatenate(
            [y[lines + 8:lines + 16] * top, y[0:lines], y[lines:lines + 8] * bottom], axis=0)
        n = lines + 16
        two = ext + pltpu.roll(ext, n - 1, 0)
        five = pltpu.roll(two, 2, 0) + (ext + pltpu.roll(two, n - 1, 0))
        return five[8:8 + lines]

    height = lines + ROWS

    def powers_of(e):
        a0 = tiles[e, 0].astype(F32)
        a1 = tiles[e, 1].astype(F32)
        p = a0 * a0 + a1 * a1
        hi = p.astype(BF16)
        lo = (p - hi.astype(F32)).astype(BF16)
        y = jnp.dot(jnp.concatenate([hi, lo], axis=0), band[...], preferred_element_type=F32)
        m = line_sums(y[0:height] + y[height:]) * (1.0 / LOOKS) + EPS
        r = 1.0 / m
        logs[e] = jnp.log(m)
        inv[e] = r * (1.0 / LOOKS)
        if e < dates:
            mean[e] = m
            term = p[0:lines, 0:cols] * r
            if e == 0:
                acc[...] = term
            else:
                acc[...] += term

    def pairs_of(e, first, last):
        def one(d, carry):
            a0 = tiles[d, 0]
            a1 = tiles[d, 1]
            b0 = tiles[e, 0]
            b1 = tiles[e, 1]
            re = a0 * b0 + a1 * b1
            im = a1 * b0 - a0 * b1
            y = jnp.dot(jnp.concatenate([re, im], axis=0), band[...], preferred_element_type=F32)
            sr = line_sums(y[0:height])
            si = line_sums(y[height:])
            coh[e, e - d - 1] = ((sr * sr + si * si) * (inv[d] * inv[e])).astype(BF16)
            return carry
        lax.fori_loop(first, last, one, 0)

    def put(src, dst, i):
        return pltpu.make_async_copy(src, dst, out_sem.at[i])

    def puts(e):
        out = [put(logs.at[e], log_out.at[e], 3 * e)]
        lo, hi = (0, e) if e < dates else (e - dates, LAG_MAX)
        if hi > lo:
            out.append(put(coh.at[e, pl.ds(lo, hi - lo)], coh_out.at[e, pl.ds(lo, hi - lo)], 3 * e + 1))
        if e < dates:
            out.append(put(mean.at[e], mean_out.at[e], 3 * e + 2))
        return out

    def stage_z(e):
        z_copy(e - dates, date - 1).wait_recv()
        x_each(e, tiles.at[e], lambda c: c.start())

    def stage_x(e):
        x_wait(e)
        a_copy(e).start()

    def stage_c(e):
        a_copy(e).wait_recv()
        powers_of(e)
        if e < dates:
            pairs_of(e, 0, e)
        else:
            pairs_of(e, e - dates, dates)
        for c in puts(e):
            c.start()

    def chain(way, to):
        return pltpu.make_async_remote_copy(
            src_ref=chain_out.at[way], dst_ref=chain_in.at[way],
            send_sem=c_send.at[way], recv_sem=c_recv.at[way],
            device_id={"date": to}, device_id_type=pl.DeviceIdType.MESH)

    def up_step(first):
        if not first:
            chain(0, date + 1).wait_recv()

        @pl.when(has_next)
        def _():
            s = acc[...] if first else acc[...] + chain_in[0].astype(F32)
            chain_out[0] = s.astype(BF16)
            chain(0, date + 1).start()

    def down_step(first):
        if not first:
            chain(1, date - 1).wait_recv()

        @pl.when(has_prev)
        def _():
            s = acc[...] if first else acc[...] + chain_in[1].astype(F32)
            chain_out[1] = s.astype(BF16)
            chain(1, date - 1).start()

    def chain_point(k, rest):
        if rest:
            pl.when(date >= k)(lambda: up_step(False))
            pl.when(date <= dates_axis - 1 - k)(lambda: down_step(False))
        else:
            pl.when(date == k)(lambda: up_step(k == 0))
            pl.when(date == dates_axis - 1 - k)(lambda: down_step(k == 0))

    def stage(f, e):
        if e < 2 * dates:
            if e < dates:
                if f is not stage_z:
                    f(e)
            else:
                pl.when(has_next)(lambda: f(e))

    for e in range(AHEAD_Z):
        stage(stage_z, e)
    for e in range(AHEAD_X):
        stage(stage_x, e)
    points = [(dates - 1) + 2 * k for k in range(1 + dates // 2)]
    for e in range(2 * dates):
        stage(stage_z, e + AHEAD_Z)
        stage(stage_x, e + AHEAD_X)
        stage(stage_c, e)
        if e in points:
            k = points.index(e)
            if k < dates_axis:
                chain_point(k, k == len(points) - 1 and k < dates_axis - 1)

    total[...] = acc[...]

    @pl.when(has_prev)
    def _():
        total[...] += chain_in[0].astype(F32)

    @pl.when(has_next)
    def _():
        total[...] += chain_in[1].astype(F32)

    total[...] = total[...] * (1.0 / float(dates * dates_axis))
    last = put(total, total_out, 6 * dates)
    last.start()

    for e in range(2 * dates):
        def done(e=e):
            for c in puts(e):
                c.wait()
            x_each(e, tiles.at[e], lambda c: c.wait_send())
            a_copy(e).wait_send()
        if e < dates:
            done()
        else:
            pl.when(has_next)(done)

    @pl.when(has_prev)
    def _():
        for k in range(dates):
            z_copy(k, date - 1).wait_send()
        chain(1, date - 1).wait_send()

    @pl.when(has_next)
    def _():
        chain(0, date + 1).wait_send()

    last.wait()


def pick_kernel(sizes, lags, coh_in, log_in, mean_in, total_in, coh_out, log_out, queg_out,
                coh, logs, ratio, mean, total, in_sem, log_sem, mean_sem, out_sem):
    dates, slots, lines, cols = sizes
    tot = pltpu.make_async_copy(total_in, total, mean_sem.at[0])
    means = pltpu.make_async_copy(mean_in, mean, mean_sem.at[1])
    loads = pltpu.make_async_copy(log_in, logs, log_sem)

    def fetch(d, s):
        lag = jnp.maximum(lags[d, s], 1)
        return pltpu.make_async_copy(coh_in.at[d + lag, lag - 1], coh.at[d, s], in_sem.at[d])

    tot.start()
    means.start()
    loads.start()

    def start(d, carry):
        for s in range(slots):
            fetch(d, s).start()
        return carry

    lax.fori_loop(0, dates, start, 0)
    tot.wait()
    means.wait()

    def queg(d, carry):
        mean[d] = mean[d] * total[...]
        return carry

    lax.fori_loop(0, dates, queg, 0)
    pltpu.make_async_copy(mean, queg_out, out_sem.at[0]).start()
    loads.wait()

    def each(d, carry):
        for s in range(slots):
            lag = lags[d, s]

            @pl.when(lag > 0)
            def _():
                ratio[d, s] = (logs[d] - logs[d + lag]).astype(BF16)

            @pl.when(lag <= 0)
            def _():
                ratio[d, s] = jnp.zeros((lines, cols), BF16)
        pltpu.make_async_copy(ratio.at[d], log_out.at[d], out_sem.at[1]).start()
        for s in range(slots):
            fetch(d, s).wait()
        for s in range(slots):
            @pl.when(lags[d, s] <= 0)
            def _():
                coh[d, s] = jnp.zeros((lines, cols), BF16)
        pltpu.make_async_copy(coh.at[d], coh_out.at[d], out_sem.at[2]).start()
        return carry

    lax.fori_loop(0, dates, each, 0)
    pltpu.make_async_copy(mean, queg_out, out_sem.at[0]).wait()
    pltpu.make_async_copy(ratio, log_out, out_sem.at[1]).wait()
    pltpu.make_async_copy(coh, coh_out, out_sem.at[2]).wait()


def solution(mesh):
    dates_axis, rng_axis, az_axis = mesh.shape["date"], mesh.shape["rng"], mesh.shape["az"]
    assert az_axis == 2 and rng_axis > 1
    sides = 1 if rng_axis == 2 else 2

    def on_device(slc, lags):
        dates, _, lines, cols = slc.shape
        slots = lags.shape[1]
        assert dates == LAG_MAX
        width = cols + sides * LANES
        anywhere = pl.BlockSpec(memory_space=pl.ANY)
        field = (lines, cols)
        dma = pltpu.SemaphoreType.DMA
        coh, logs, mean, total = pl.pallas_call(
            functools.partial(gather_kernel, (dates_axis, rng_axis, dates, lines, cols)),
            out_shape=[
                jax.ShapeDtypeStruct((2 * dates, LAG_MAX, *field), BF16),
                jax.ShapeDtypeStruct((2 * dates, *field), F32),
                jax.ShapeDtypeStruct((dates, *field), F32),
                jax.ShapeDtypeStruct(field, F32),
            ],
            in_specs=[anywhere],
            out_specs=[anywhere] * 4,
            scratch_shapes=[
                pltpu.VMEM((2 * dates, 2, lines + ROWS, width), BF16),
                pltpu.VMEM((width, cols), BF16),
                pltpu.VMEM((2 * dates, LAG_MAX, *field), BF16),
                pltpu.VMEM((2 * dates, *field), F32),
                pltpu.VMEM((2 * dates, *field), F32),
                pltpu.VMEM((dates, *field), F32),
                pltpu.VMEM(field, F32),
                pltpu.VMEM(field, F32),
                pltpu.VMEM((2, *field), BF16),
                pltpu.VMEM((2, *field), BF16),
                dma, dma((dates,)), dma((dates,)),
                dma((sides, 2 * dates)), dma((sides, 2 * dates)),
                dma((2 * dates,)), dma((2 * dates,)),
                dma((2,)), dma((2,)), dma((6 * dates + 1,)),
            ],
            compiler_params=pltpu.CompilerParams(collective_id=0, has_side_effects=True),
            name="gather",
        )(slc)
        return pl.pallas_call(
            functools.partial(pick_kernel, (dates, slots, lines, cols)),
            out_shape=[
                jax.ShapeDtypeStruct((dates, slots, *field), BF16),
                jax.ShapeDtypeStruct((dates, slots, *field), BF16),
                jax.ShapeDtypeStruct((dates, *field), F32),
            ],
            in_specs=[pl.BlockSpec(memory_space=pltpu.SMEM)] + [anywhere] * 4,
            out_specs=[anywhere] * 3,
            scratch_shapes=[
                pltpu.VMEM((dates, slots, *field), BF16),
                pltpu.VMEM((2 * dates, *field), F32),
                pltpu.VMEM((dates, slots, *field), BF16),
                pltpu.VMEM((dates, *field), F32),
                pltpu.VMEM(field, F32),
                dma((dates,)), dma, dma((2,)), dma((3,)),
            ],
            name="pick",
        )(lags, coh, logs, mean, total)

    return jax.shard_map(
        on_device,
        mesh=mesh,
        in_specs=(P(("slab", "date"), None, "az", "rng"), P("date", None)),
        out_specs=(
            P(("slab", "date"), None, "az", "rng"),
            P(("slab", "date"), None, "az", "rng"),
            P(("slab", "date"), "az", "rng"),
        ),
        check_vma=False,
    )
```

```python
import functools

import jax
import jax.numpy as jnp
from jax import lax
from jax.experimental import pallas as pl
from jax.experimental.pallas import tpu as pltpu
from jax.sharding import PartitionSpec as P

HALF_AZ = 2
HALF_RG = 10
LAG_MAX = 8
EPS = 1e-05
LOOKS = float((2 * HALF_AZ + 1) * (2 * HALF_RG + 1))

LANES = 128
ROWS = 16
FLIGHT = 8
BATCH = 4
VMEM_BYTES = 67043328
AHEAD_Z = 5
AHEAD_X = 2
F32 = jnp.float32
BF16 = jnp.bfloat16


def order_of(dates):
    words = ["S%d" % k for k in range(dates)] + ["X%d" % e for e in range(AHEAD_X)]
    points = [(dates - 1) + 2 * k for k in range(dates // 2)]
    for e in range(2 * dates):
        if dates <= e + AHEAD_Z < 2 * dates:
            words.append("Z%d" % (e + AHEAD_Z))
        if e + AHEAD_X < 2 * dates:
            words.append("X%d" % (e + AHEAD_X))
        words += ["A%d" % e, "P%d" % e]
        if e:
            words.append("Q%d" % e)
        if e in points:
            words.append("K%d" % points.index(e))
    return words


def gather_kernel(sizes, slc, lags_in, coh, logs, mean, total, lags,
                  tiles, band, pick, inv, acc, chain_out, chain_in,
                  own_sem, z_send, z_recv, x_send, x_recv, a_send, a_recv,
                  c_send, c_recv, lag_sem):
    dates_axis, rng_axis, dates, lines, cols = sizes
    sides = 1 if rng_axis == 2 else 2
    date = lax.axis_index("date")
    rng = lax.axis_index("rng")
    az = lax.axis_index("az")
    has_next = date < dates_axis - 1
    has_prev = date > 0
    has_right = rng < rng_axis - 1
    has_left = rng > 0
    peer = 1 - az
    center = (slice(None), pl.ds(0, lines), pl.ds(0, cols))

    own = pltpu.make_async_copy(
        slc, tiles.at[pl.ds(0, dates), :, pl.ds(0, lines), pl.ds(0, cols)], own_sem)
    own.start()
    lag_copy = pltpu.make_async_copy(lags_in, lags, lag_sem)
    lag_copy.start()

    barrier = pltpu.get_barrier_semaphore()

    def greet(where):
        pl.semaphore_signal(barrier, inc=1, device_id=where, device_id_type=pl.DeviceIdType.MESH)

    greet({"az": peer})
    pl.when(has_prev)(lambda: greet({"date": date - 1}))
    pl.when(has_next)(lambda: greet({"date": date + 1}))
    pl.when(has_left)(lambda: greet({"rng": rng - 1}))
    pl.when(has_right)(lambda: greet({"rng": rng + 1}))

    col_out = lax.broadcasted_iota(jnp.int32, (cols, cols), 1)
    col_in = lax.broadcasted_iota(jnp.int32, (cols, cols), 0)
    band[0:cols, :] = (jnp.abs(col_in - col_out) <= HALF_RG).astype(F32).astype(BF16)
    edge_in = lax.broadcasted_iota(jnp.int32, (LANES, cols), 0)
    edge_out = lax.broadcasted_iota(jnp.int32, (LANES, cols), 1)
    for side in range(sides):
        if sides == 1:
            shift = (1 - rng) * cols - rng * LANES
        else:
            shift = -LANES if side == 0 else cols
        near = jnp.abs(edge_in + shift - edge_out) <= HALF_RG
        band[cols + side * LANES:cols + (side + 1) * LANES, :] = near.astype(F32).astype(BF16)

    peers = 1
    for cond in (has_prev, has_next, has_left, has_right):
        peers = peers + cond.astype(jnp.int32)
    pl.semaphore_wait(barrier, peers)

    def x_copy(e, src, side, to, start_col):
        block = cols + side * LANES
        if not isinstance(start_col, int):
            start_col = pl.multiple_of(start_col, LANES)
        return pltpu.make_async_remote_copy(
            src_ref=src.at[:, pl.ds(0, lines), pl.ds(start_col, LANES)],
            dst_ref=tiles.at[e, :, pl.ds(0, lines), pl.ds(block, LANES)],
            send_sem=x_send.at[side, e], recv_sem=x_recv.at[side, e],
            device_id={"rng": to}, device_id_type=pl.DeviceIdType.MESH)

    def x_each(e, src, act):
        if sides == 1:
            act(x_copy(e, src, 0, 1 - rng, (1 - rng) * (cols - LANES)))
        else:
            pl.when(has_right)(lambda: act(x_copy(e, src, 0, rng + 1, cols - LANES)))
            pl.when(has_left)(lambda: act(x_copy(e, src, 1, rng - 1, 0)))

    def x_wait(e):
        src = tiles.at[e]
        if sides == 1:
            x_copy(e, src, 0, 1 - rng, 0).wait_recv()
        else:
            pl.when(has_left)(lambda: x_copy(e, src, 0, rng - 1, 0).wait_recv())
            pl.when(has_right)(lambda: x_copy(e, src, 1, rng + 1, 0).wait_recv())

    row_src = (1 - az) * (lines - ROWS)

    def a_copy(e):
        return pltpu.make_async_remote_copy(
            src_ref=tiles.at[e, :, pl.ds(pl.multiple_of(row_src, ROWS), ROWS), :],
            dst_ref=tiles.at[e, :, pl.ds(lines, ROWS), :],
            send_sem=a_send.at[e], recv_sem=a_recv.at[e],
            device_id={"az": peer}, device_id_type=pl.DeviceIdType.MESH)

    def z_copy(k, to):
        return pltpu.make_async_remote_copy(
            src_ref=slc.at[k], dst_ref=tiles.at[(dates + k, *center)],
            send_sem=z_send.at[k], recv_sem=z_recv.at[k],
            device_id={"date": to}, device_id_type=pl.DeviceIdType.MESH)

    for k in range(dates):
        x_each(k, slc.at[k], lambda c: c.start())

    if sides == 2:
        zeros = jnp.zeros((2 * dates, 2, lines, LANES), BF16)

        @pl.when(rng == 0)
        def _():
            tiles[:, :, 0:lines, cols:cols + LANES] = zeros

        @pl.when(rng == rng_axis - 1)
        def _():
            tiles[:, :, 0:lines, cols + LANES:cols + 2 * LANES] = zeros

    @pl.when(date == dates_axis - 1)
    def _():
        tiles[dates:] = jnp.zeros((dates, 2, lines + ROWS, cols + sides * LANES), BF16)

    own.wait()

    height = lines + ROWS
    width = cols + sides * LANES
    line_out = lax.broadcasted_iota(jnp.int32, (lines, height), 0)
    row = lax.broadcasted_iota(jnp.int32, (lines, height), 1)
    line_in = row - jnp.where(row >= lines, az * height, 0)
    pick[...] = (jnp.abs(line_in - line_out) <= HALF_AZ).astype(F32).astype(BF16)

    def line_sums(left, right):
        return jnp.dot(pick[...], jnp.concatenate([left, right], axis=1), preferred_element_type=F32)

    def column_sums(rows):
        return jnp.dot(jnp.concatenate(rows, axis=0), band[...], preferred_element_type=F32)

    def halves(x):
        hi = x.astype(BF16)
        return hi, (x - hi.astype(F32)).astype(BF16)

    def powers_of(e):
        a0 = tiles[e, 0].astype(F32)
        a1 = tiles[e, 1].astype(F32)
        p = a0 * a0 + a1 * a1
        z = jnp.dot(jnp.concatenate([pick[...]] * 2, axis=1), jnp.concatenate(halves(p), axis=0),
                    preferred_element_type=F32)
        y = column_sums(halves(z))
        m = (y[0:lines] + y[lines:]) * (1.0 / LOOKS) + EPS
        r = 1.0 / m
        logs[e] = jnp.log(m)
        inv[e] = r * (1.0 / LOOKS)
        if e < dates:
            mean[e] = m
            term = p[0:lines, 0:cols] * r
            if e == 0:
                acc[...] = term
            else:
                acc[...] += term

    def pairs_of(e, first, last):
        for start in range(first, last, BATCH):
            group = range(start, min(start + BATCH, last))
            sums = []
            for d in group:
                a0 = tiles[d, 0]
                a1 = tiles[d, 1]
                b0 = tiles[e, 0]
                b1 = tiles[e, 1]
                z = line_sums(a0 * b0 + a1 * b1, a1 * b0 - a0 * b1).astype(BF16)
                sums += [z[:, 0:width], z[:, width:]]
            y = column_sums(sums)
            for i, d in enumerate(group):
                sr = y[2 * i * lines:(2 * i + 1) * lines]
                si = y[(2 * i + 1) * lines:(2 * i + 2) * lines]
                coh[e, e - d - 1] = ((sr * sr + si * si) * (inv[d] * inv[e])).astype(BF16)

    def stage_s(k):
        @pl.when(has_prev)
        def _():
            if k >= FLIGHT:
                z_copy(k - FLIGHT, date - 1).wait_send()
            z_copy(k, date - 1).start()

    def stage_z(e):
        z_copy(e - dates, date - 1).wait_recv()
        x_each(e, tiles.at[e], lambda c: c.start())

    def stage_x(e):
        x_wait(e)
        a_copy(e).start()

    def stage_a(e):
        a_copy(e).wait_recv()

    def stage_q(e):
        if e < dates:
            pairs_of(e, 0, e)
        else:
            pairs_of(e, e - dates, dates)

    def chain(way, to):
        return pltpu.make_async_remote_copy(
            src_ref=chain_out.at[way], dst_ref=chain_in.at[way],
            send_sem=c_send.at[way], recv_sem=c_recv.at[way],
            device_id={"date": to}, device_id_type=pl.DeviceIdType.MESH)

    def up_step(first):
        if not first:
            chain(0, date + 1).wait_recv()

        @pl.when(has_next)
        def _():
            s = acc[...] if first else acc[...] + chain_in[0].astype(F32)
            chain_out[0] = s.astype(BF16)
            chain(0, date + 1).start()

    def down_step(first):
        if not first:
            chain(1, date - 1).wait_recv()

        @pl.when(has_prev)
        def _():
            s = acc[...] if first else acc[...] + chain_in[1].astype(F32)
            chain_out[1] = s.astype(BF16)
            chain(1, date - 1).start()

    def chain_point(k, rest):
        if rest:
            pl.when(date >= k)(lambda: up_step(False))
            pl.when(date <= dates_axis - 1 - k)(lambda: down_step(False))
        else:
            pl.when(date == k)(lambda: up_step(k == 0))
            pl.when(date == dates_axis - 1 - k)(lambda: down_step(k == 0))

    stages = {"S": stage_s, "Z": stage_z, "X": stage_x, "A": stage_a, "P": powers_of, "Q": stage_q}
    words = order_of(dates)
    points = sum(word[0] == "K" for word in words)
    todo = [(word[0], int(word[1:])) for word in words]
    while todo:
        kind, e = todo.pop(0)
        if kind == "K":
            if e < dates_axis:
                chain_point(e, e == points - 1)
        elif e < dates or kind in "PQ":
            stages[kind](e)
        else:
            run = [(kind, e)]
            while todo and todo[0][0] in "ZXA" and todo[0][1] >= dates:
                run.append(todo.pop(0))

            @pl.when(has_next)
            def _():
                for name, i in run:
                    stages[name](i)

    total[...] = acc[...]

    @pl.when(has_prev)
    def _():
        total[...] += chain_in[0].astype(F32)

    @pl.when(has_next)
    def _():
        total[...] += chain_in[1].astype(F32)

    total[...] = total[...] * (1.0 / float(dates * dates_axis))

    lag_copy.wait()
    for e in range(2 * dates):
        def done(e=e):
            x_each(e, tiles.at[e], lambda c: c.wait_send())
            a_copy(e).wait_send()
        if e < dates:
            done()
        else:
            pl.when(has_next)(done)

    @pl.when(has_prev)
    def _():
        for k in range(dates - FLIGHT, dates):
            z_copy(k, date - 1).wait_send()
        chain(1, date - 1).wait_send()

    @pl.when(has_next)
    def _():
        chain(0, date + 1).wait_send()


def pick_kernel(sizes, lags_in, coh, logs, mean, total, coh_out, log_out, queg_out,
                lags, zero, ratio, queg, lag_sem, coh_sem, log_sem, queg_sem):
    dates, slots, lines, cols = sizes
    lag_copy = pltpu.make_async_copy(lags_in, lags, lag_sem)
    lag_copy.start()
    zero[...] = jnp.zeros((lines, cols), BF16)

    def start(d, carry):
        for s in range(slots):
            lag = lags[d, s]

            @pl.when(lag > 0)
            def _():
                pltpu.make_async_copy(coh.at[d + lag, lag - 1], coh_out.at[d, s], coh_sem).start()

            @pl.when(lag <= 0)
            def _():
                pltpu.make_async_copy(zero, coh_out.at[d, s], coh_sem).start()
        return carry

    def filtered(d, carry):
        queg[d] = mean[d] * total[...]
        pltpu.make_async_copy(queg.at[d], queg_out.at[d], queg_sem).start()
        return carry

    lax.fori_loop(0, dates, filtered, 0)
    lag_copy.wait()
    lax.fori_loop(0, dates, start, 0)

    def each(d, carry):
        for s in range(slots):
            lag = lags[d, s]
            there = d + jnp.maximum(lag, 0)
            keep = jnp.broadcast_to(lag > 0, (lines, cols))
            ratio[d, s] = jnp.where(keep, logs[d] - logs[there], 0.0).astype(BF16)
        pltpu.make_async_copy(ratio.at[d], log_out.at[d], log_sem).start()
        return carry

    lax.fori_loop(0, dates, each, 0)
    pltpu.make_async_copy(ratio, coh_out, coh_sem).wait()
    pltpu.make_async_copy(ratio, log_out, log_sem).wait()
    pltpu.make_async_copy(queg, queg_out, queg_sem).wait()


def solution(mesh):
    dates_axis, rng_axis, az_axis = mesh.shape["date"], mesh.shape["rng"], mesh.shape["az"]
    assert az_axis == 2 and rng_axis > 1
    sides = 1 if rng_axis == 2 else 2

    def on_device(slc, lags):
        dates, _, lines, cols = slc.shape
        slots = lags.shape[1]
        held = 4 * lines * cols * (LAG_MAX * dates + 3 * dates + 1) + 50 * 2 ** 20
        assert dates == LAG_MAX
        width = cols + sides * LANES
        inside = pl.BlockSpec(memory_space=pltpu.VMEM)
        anywhere = pl.BlockSpec(memory_space=pltpu.HBM)
        field = (lines, cols)
        dma = pltpu.SemaphoreType.DMA
        coh, logs, mean, total, lags = pl.pallas_call(
            functools.partial(gather_kernel, (dates_axis, rng_axis, dates, lines, cols)),
            out_shape=[
                jax.ShapeDtypeStruct((2 * dates, LAG_MAX, *field), BF16),
                jax.ShapeDtypeStruct((2 * dates, *field), F32),
                jax.ShapeDtypeStruct((dates, *field), F32),
                jax.ShapeDtypeStruct(field, F32),
                jax.ShapeDtypeStruct(lags.shape, lags.dtype),
            ],
            in_specs=[anywhere] * 2,
            out_specs=[inside] * 5,
            scratch_shapes=[
                pltpu.VMEM((2 * dates, 2, lines + ROWS, width), BF16),
                pltpu.VMEM((width, cols), BF16),
                pltpu.VMEM((lines, lines + ROWS), BF16),
                pltpu.VMEM((2 * dates, *field), F32),
                pltpu.VMEM(field, F32),
                pltpu.VMEM((2, *field), BF16),
                pltpu.VMEM((2, *field), BF16),
                dma, dma((dates,)), dma((dates,)),
                dma((sides, 2 * dates)), dma((sides, 2 * dates)),
                dma((2 * dates,)), dma((2 * dates,)),
                dma((2,)), dma((2,)), dma,
            ],
            compiler_params=pltpu.CompilerParams(collective_id=0, has_side_effects=True, vmem_limit_bytes=VMEM_BYTES - held),
            name="gather",
        )(slc, lags)
        return pl.pallas_call(
            functools.partial(pick_kernel, (dates, slots, lines, cols)),
            out_shape=[
                jax.ShapeDtypeStruct((dates, slots, *field), BF16),
                jax.ShapeDtypeStruct((dates, slots, *field), BF16),
                jax.ShapeDtypeStruct((dates, *field), F32),
            ],
            in_specs=[inside] * 5,
            out_specs=[anywhere] * 3,
            scratch_shapes=[
                pltpu.SMEM((dates, slots), jnp.int32),
                pltpu.VMEM(field, BF16),
                pltpu.VMEM((dates, slots, *field), BF16),
                pltpu.VMEM((dates, *field), F32),
                dma, dma, dma, dma,
            ],
            compiler_params=pltpu.CompilerParams(vmem_limit_bytes=16 * 2 ** 20),
            name="pick",
        )(lags, coh, logs, mean, total)

    return jax.shard_map(
        on_device,
        mesh=mesh,
        in_specs=(P(("slab", "date"), None, "az", "rng"), P("date", None)),
        out_specs=(
            P(("slab", "date"), None, "az", "rng"),
            P(("slab", "date"), None, "az", "rng"),
            P(("slab", "date"), "az", "rng"),
        ),
        check_vma=False,
    )
```
